32 devices in a mesh: row: 4 (over y, x), col: 8 (over z, core).
Axes of the slice: x: 2, y: 2, z: 4, core: 2. Of those that a mesh axis runs over, the one named last changes fastest.
Arguments:
- tokens: bfloat16 [32, 512, 960], P(('row', 'col')), may hold values from -6 to 6
- segment_ids: int32 [32, 512], P(('row', 'col')), may hold values from 0 to 3, never falling along the last dimension, each value on 1 to 320 neighbouring positions
- route_one: int32 [32, 384], P(('row', 'col')), may hold values from 0 to 511, as said below
- route_two: int32 [32, 256], P(('row', 'col')), may hold values from 0 to 511, as said below
- route_three: int32 [32, 128], P(('row', 'col')), may hold values from 0 to 511, as said below
- attn_gain: bfloat16 [960], P('row'), may hold values from 0.5 to 1.5
- router: bfloat16 [960, 3], P('row'), may hold values from -0.125 to 0.125
- w_query: bfloat16 [960, 960], P('row', 'col'), may hold values from -0.1875 to 0.1875
- w_key: bfloat16 [960, 320], P('row', 'col'), may hold values from -0.1875 to 0.1875
- w_value: bfloat16 [960, 320], P('row', 'col'), may hold values from -0.1875 to 0.1875
- w_out: bfloat16 [960, 960], P('row', 'col'), may hold values from -0.75 to 0.75
- ffn_gain: bfloat16 [960], P('row'), may hold values from 0.5 to 1.5
- w_gate: bfloat16 [960, 2560], P('row', 'col'), may hold values from -0.1875 to 0.1875
- w_up: bfloat16 [960, 2560], P('row', 'col'), may hold values from -0.1875 to 0.1875
- w_down: bfloat16 [2560, 960], P('row', 'col'), may hold values from -0.125 to 0.125
- cotangent: bfloat16 [32, 512, 960], P(('row', 'col')), may hold values from -6 to 6
Outputs:
- output: bfloat16 [32, 512, 960], P(('row', 'col'))
- token_grad: bfloat16 [32, 512, 960], P(('row', 'col'))
- attn_gain_grad: float32 [960], P('row')
- router_grad: float32 [960, 3], P('row')
- w_query_grad: float32 [960, 960], P('row', 'col')
- w_key_grad: float32 [960, 320], P('row', 'col')
- w_value_grad: float32 [960, 320], P('row', 'col')
- w_out_grad: float32 [960, 960], P('row', 'col')
- ffn_gain_grad: float32 [960], P('row')
- w_gate_grad: float32 [960, 2560], P('row', 'col')
- w_up_grad: float32 [960, 2560], P('row', 'col')
- w_down_grad: float32 [2560, 960], P('row', 'col')
The draws below stay inside these ranges and needn't reach their ends.
Inputs may be any that keep to these rules, and one draw needn't show every extreme that they name: `segment_ids`: along a row the segment ids never fall; equal ids mark one document. `route_one`: each row holds 384 distinct positions of its sequence in ascending order. `route_two`: each row holds 256 distinct positions in ascending order, all in the same row of route_one. `route_three`: each row holds 128 distinct positions in ascending order, all in the same row of route_two.
All inputs are finite; a program needn't handle non-finite values.
Results may differ from the reference program's by a relative error of at most 0.028.
Values may be sent and summed in bfloat16 or wider, within the bound.
No kernel may reach another device: no remote copies, remote signals or barrier semaphores. Data moves between devices by JAX's collectives and lax.ppermute only.
A program may use at most 192 MiB of HBM per device.

```python
import math
import jax
import jax.numpy as jnp
import numpy as np
from jax import lax

D = 960
HEADS = 15
KV_HEADS = 5
HEAD_DIM = 64
FF = 2560
STEPS = 3
LEN = 512
QW = 960
KVW = 320
C1 = 384
C2 = 256
C3 = 128
SEQS = 32


def route_order(key):
    keys = jax.random.split(jax.random.fold_in(key, 11), SEQS)
    return jax.vmap(lambda item_key: jax.random.permutation(item_key, LEN))(keys)


def draw_route_one(key, part):
    return jnp.sort(route_order(key)[:, :C1], axis=1).astype(jnp.int32)


def draw_route_two(key, part):
    return jnp.sort(route_order(key)[:, :C2], axis=1).astype(jnp.int32)


def draw_route_three(key, part):
    return jnp.sort(route_order(key)[:, :C3], axis=1).astype(jnp.int32)


def with_spikes(array, rng, source, target, blocks, factor):
    def block_of(position):
        return (jnp.arange(array.shape[position]) // (array.shape[position] // blocks)).reshape((-1,) + (1,) * (array.ndim - 1 - position))

    one_side = jax.random.permutation(rng, blocks)[block_of(target)]
    other_side = (block_of(target) + blocks // 2) % blocks
    return jnp.where((block_of(source) == one_side) | (block_of(source) == other_side), factor * array, array)


def block_levels(stream_key, extent, cuts, smallest, largest):
    level, own = 1.0, jax.random.fold_in(stream_key, 6)
    for position, blocks in cuts:
        draws = jnp.exp(jax.random.uniform(jax.random.fold_in(own, position), (blocks,), jnp.float32, smallest / len(cuts), largest / len(cuts)))
        level = level * jnp.repeat(draws, extent[position] // blocks).reshape([-1 if axis == position else 1 for axis in range(len(extent))])
    return level


def length_profile(amount, total, limit, skew):
    weights = [(1 << 20) // math.isqrt(rank ** skew) + 1 for rank in range(2, amount + 1)]
    surplus, holding = total - limit - (amount - 1), [1] * (amount - 1)
    while surplus > 0:
        candidates = [i for i in range(amount - 1) if holding[i] < limit]
        pool, budget = sum([weights[i] for i in candidates]), surplus
        for i in candidates:
            addition = min(limit - holding[i], max(1, budget * weights[i] // pool), surplus)
            holding[i] = holding[i] + addition
            surplus = surplus - addition
    return np.array([limit] + holding)


def uneven(key, count, total, reach, lean):
    if count == 2:
        one = jax.random.randint(key, (), max(1, total - reach), min(reach, total - 1) + 1)
        return jnp.stack([one, total - one])
    sizes = jnp.asarray(length_profile(count, total, reach, lean), jnp.int32)
    couples = (count - 1) // 2
    giver, sink = sizes[1:1 + 2 * couples:2], sizes[2:2 + 2 * couples:2]
    margin = jnp.minimum(giver - 1, reach - sink)
    shifted = jax.random.randint(jax.random.fold_in(key, 1), (couples,), 0, 1 << 20) % (margin + 1)
    sizes = sizes.at[1:1 + 2 * couples:2].set(giver - shifted).at[2:2 + 2 * couples:2].set(sink + shifted)
    return sizes[jax.random.permutation(jax.random.fold_in(key, 2), count)]


def normal_values(stream_key, extent, width, most, shards=(), kind=jnp.bfloat16):
    entries = jax.random.normal(stream_key, extent, jnp.float32) * width
    if len(shards) > 0:
        entries = block_levels(stream_key, extent, shards, -0.22, 0.18) * entries
    return jnp.clip(entries, min=-most, max=most).astype(kind)


def gaussian_with(own_key, dims, deviation, bound, cuts, heavy, kind=jnp.bfloat16):
    entries = deviation * jax.random.normal(own_key, dims, jnp.float32)
    if cuts:
        entries = entries * block_levels(own_key, dims, cuts, -0.22, 0.18)
    return jnp.clip(with_spikes(entries, jax.random.fold_in(own_key, 3), *heavy), -bound, bound).astype(kind)


def setup_inputs(seed: int = 0) -> dict:
    arg_keys = jax.random.split(jax.random.key(seed), 17)
    tokens = normal_values(arg_keys[0], (SEQS, LEN, D), 1.0, 6.0, ((0, 32),))
    segment_ids = jax.vmap(lambda own: jnp.searchsorted(jnp.cumsum(uneven(own, max(2, LEN // 128), LEN, LEN // 2 + LEN // 8, 1)), jnp.arange(LEN), side="right"))(jax.random.split(arg_keys[1], SEQS)).reshape((SEQS, LEN)).astype(jnp.int32)
    route_one = draw_route_one(jax.random.fold_in(arg_keys[16], 71), 0)
    route_two = draw_route_two(jax.random.fold_in(arg_keys[16], 71), 0)
    route_three = draw_route_three(jax.random.fold_in(arg_keys[16], 71), 0)
    attn_gain = jnp.clip(1.0 + 0.1 * jax.random.normal(arg_keys[5], (D,), jnp.float32), 0.5, 1.5).astype(jnp.bfloat16)
    router = normal_values(arg_keys[6], (D, STEPS), (2 * D) ** -0.5, 0.125, ((0, 4),))
    w_query = normal_values(arg_keys[7], (D, QW), D ** -0.5, 0.1875, ((0, 4), (1, 8)))
    w_key = normal_values(arg_keys[8], (D, KVW), D ** -0.5, 0.1875, ((0, 4), (1, 8)))
    w_value = normal_values(arg_keys[9], (D, KVW), D ** -0.5, 0.1875, ((0, 4), (1, 8)))
    w_out = normal_values(arg_keys[10], (QW, D), (QW // 16) ** -0.5, 0.75, ((0, 4), (1, 8)))
    ffn_gain = jnp.clip(1.0 + 0.1 * jax.random.normal(arg_keys[11], (D,), jnp.float32), 0.5, 1.5).astype(jnp.bfloat16)
    w_gate = normal_values(arg_keys[12], (D, FF), D ** -0.5, 0.1875, ((0, 4), (1, 8)))
    w_up = normal_values(arg_keys[13], (D, FF), D ** -0.5, 0.1875, ((0, 4), (1, 8)))
    w_down = normal_values(arg_keys[14], (FF, D), FF ** -0.5, 0.125, ((0, 4), (1, 8)))
    cotangent = gaussian_with(arg_keys[15], (SEQS, LEN, D), 1.0, 6.0, ((0, 32),), (0, 2, 32, 2.75))
    return {"tokens": tokens, "segment_ids": segment_ids, "route_one": route_one, "route_two": route_two, "route_three": route_three, "attn_gain": attn_gain, "router": router, "w_query": w_query, "w_key": w_key, "w_value": w_value, "w_out": w_out, "ffn_gain": ffn_gain, "w_gate": w_gate, "w_up": w_up, "w_down": w_down, "cotangent": cotangent}


@jax.custom_vjp
def low(v):
    return lax.optimization_barrier(v.astype(jnp.bfloat16)).astype(jnp.float32)

@jax.custom_vjp
def low_back(v):
    return v

def low_keep(v):
    return (low(v), None)

def low_pass(kept, grad):
    return (grad,)

def back_keep(v):
    return (v, None)

def back_low(kept, grad):
    return (low(grad),)
low.defvjp(low_keep, low_pass)
low_back.defvjp(back_keep, back_low)
highest = lax.Precision.HIGHEST
eps_norm = 1e-05
rope_base = 10000.0

def rms_scale(values, gain_vec):
    return values * lax.rsqrt(lax.optimization_barrier(jnp.mean(values * values, axis=-1, keepdims=True)) + eps_norm) * gain_vec

def positions_of(segment_row):
    length = segment_row.shape[0]
    places = jnp.arange(length, dtype=jnp.int32)
    earlier = (segment_row[None, :] == segment_row[:, None]) & (places[None, :] < places[:, None])
    return lax.optimization_barrier(jnp.sum(earlier.astype(jnp.int32), axis=1)).astype(jnp.int32)

def rotary_tables(places):
    half_dim = HEAD_DIM // 2
    inverse = rope_base ** (-(jnp.arange(half_dim, dtype=jnp.float32) * 2.0 / HEAD_DIM))
    angles = places.astype(jnp.float32)[:, None] * inverse[None, :]
    return (jnp.cos(angles), jnp.sin(angles))

def rotate(values, cosine, sine_table):
    half_dim = values.shape[-1] // 2
    first_half = values[..., :half_dim]
    second = values[..., half_dim:]
    return jnp.concatenate([first_half * cosine - second * sine_table, second * cosine + first_half * sine_table], axis=-1)

def block_step(stream, chosen, segment_row, place_row, router_col, weight_set):
    w_query, w_key, w_value, w_out, attn_gain, w_gate, w_up, w_down, ffn_gain = weight_set
    rows_picked = chosen.shape[0]
    groups = HEADS // KV_HEADS
    picked = stream[chosen]
    gate_value = jax.nn.sigmoid(jnp.dot(picked, router_col, precision=highest))
    normed = low(rms_scale(picked, attn_gain))
    query_raw = low_back(jnp.dot(normed, w_query, precision=highest))
    key_raw = low_back(jnp.dot(normed, w_key, precision=highest))
    value_low = low(low_back(jnp.dot(normed, w_value, precision=highest)))
    cosine, sine_table = rotary_tables(place_row[chosen])
    query_rot = low(rotate(query_raw.reshape(rows_picked, KV_HEADS, groups, HEAD_DIM), cosine[:, None, None, :], sine_table[:, None, None, :]))
    key_rot = low(rotate(key_raw.reshape(rows_picked, KV_HEADS, HEAD_DIM), cosine[:, None, :], sine_table[:, None, :]))
    value_heads = value_low.reshape(rows_picked, KV_HEADS, HEAD_DIM)
    segment_pick = segment_row[chosen]
    allowed = (segment_pick[None, :] == segment_pick[:, None]) & (chosen[None, :] <= chosen[:, None])
    scores = low_back(jnp.einsum('qkgd,skd->kgqs', query_rot, key_rot, precision=highest) * HEAD_DIM ** (-0.5))
    masked = jnp.where(allowed, scores, -1e+30)
    prob_low = low(jax.nn.softmax(masked, axis=-1))
    mixed = jnp.einsum('kgqs,skd->qkgd', prob_low, value_heads, precision=highest)
    mixed_low = low(low_back(mixed.reshape(rows_picked, HEADS * HEAD_DIM)))
    attn_out = low_back(jnp.dot(mixed_low, w_out, precision=highest))
    middle = picked + attn_out
    normed_two = low(rms_scale(middle, ffn_gain))
    gate_raw = low_back(jnp.dot(normed_two, w_gate, precision=highest))
    up_raw = low_back(jnp.dot(normed_two, w_up, precision=highest))
    hidden = low(jax.nn.silu(gate_raw) * up_raw)
    ffn_out = low_back(jnp.dot(hidden, w_down, precision=highest))
    updated = picked + gate_value[:, None] * (attn_out + ffn_out)
    return stream.at[chosen].set(updated)

def reference(tokens, segment_ids, route_one, route_two, route_three, attn_gain, router, w_query, w_key, w_value, w_out, ffn_gain, w_gate, w_up, w_down, cotangent):
    floats = [tokens, attn_gain, router, w_query, w_key, w_value, w_out, ffn_gain, w_gate, w_up, w_down]
    floats = [array_in.astype(jnp.float32) for array_in in floats]

    def forward(tokens_f, attn_gain_f, router_f, query_f, key_f, value_f, out_f, ffn_gain_f, gate_f, up_f, down_f):
        weight_set = (query_f, key_f, value_f, out_f, attn_gain_f, gate_f, up_f, down_f, ffn_gain_f)

        def one_sequence(pieces):
            row_tokens, segment_row, pick_one, pick_two, pick_three = pieces
            place_row = positions_of(segment_row)
            stream = row_tokens
            for step_index, chosen in enumerate((pick_one, pick_two, pick_three)):
                stream = block_step(stream, chosen, segment_row, place_row, router_f[:, step_index], weight_set)
            return stream
        return lax.map(jax.checkpoint(one_sequence), (tokens_f, segment_ids, route_one, route_two, route_three))
    result, pullback = jax.vjp(forward, *floats)
    grads = pullback(cotangent.astype(jnp.float32))
    return (result.astype(jnp.bfloat16), grads[0].astype(jnp.bfloat16), grads[1], grads[2], grads[3], grads[4], grads[5], grads[6], grads[7], grads[8], grads[9], grads[10])
```

```python
import jax
import jax.numpy as jnp
from jax import lax
from jax.sharding import PartitionSpec as P

HEADS = 15
KV_HEADS = 5
GROUPS = 3
HEAD_DIM = 64
STEPS = 3
EPS = 1e-05
ROPE_BASE = 10000.0
SCALE = HEAD_DIM ** (-0.5)
F32 = jnp.float32
BF16 = jnp.bfloat16
highest = lax.Precision.HIGHEST


def dot(a, b):
    return jnp.dot(a, b, preferred_element_type=F32)


def dot_nt(a, b):
    return lax.dot_general(a, b, (((1,), (1,)), ((), ())), preferred_element_type=F32)


def dot_tn(a, b):
    return lax.dot_general(a, b, (((0,), (0,)), ((), ())), preferred_element_type=F32)


def rms(values):
    return lax.rsqrt(jnp.mean(values * values, axis=-1, keepdims=True) + EPS)


def rms_back(values, inverse, gain, grad):
    scaled = grad * gain
    inner = jnp.mean(scaled * values, axis=-1, keepdims=True)
    return inverse * scaled - values * (inverse * inverse * inverse * inner)


def rotate(values, cosine, sine):
    half = HEAD_DIM // 2
    a, b = values[..., :half], values[..., half:]
    return jnp.concatenate([a * cosine - b * sine, b * cosine + a * sine], axis=-1)


def token_order(segment_row, routes):
    length = segment_row.shape[0]
    places = jnp.arange(length, dtype=jnp.int32)
    level = jnp.zeros((length,), jnp.int32)
    for route in routes:
        level = level + jnp.sum((route[:, None] == places[None, :]).astype(jnp.int32), axis=0)
    before = (level[:, None] > level[None, :]) | (
        (level[:, None] == level[None, :]) & (places[:, None] < places[None, :])
    )
    spot = jnp.sum(before.astype(jnp.int32), axis=0)
    earlier = (segment_row[:, None] == segment_row[None, :]) & (places[:, None] < places[None, :])
    place = jnp.sum(earlier.astype(jnp.int32), axis=0)
    chosen = spot[None, :] == places[:, None]
    zero = jnp.int32(0)
    pick = lambda v: jnp.sum(jnp.where(chosen, v[None, :], zero), axis=1)
    return chosen.astype(BF16), pick(places), pick(segment_row), pick(place)


def pack_small(attn_gain, router, ffn_gain, width):
    flat = jnp.concatenate([attn_gain[:, None], router, ffn_gain[:, None]], axis=1).reshape(-1)
    rows = -(-flat.shape[0] // width)
    rows = -(-rows // 8) * 8
    return jnp.pad(flat, (0, rows * width - flat.shape[0])).reshape(rows, width)


def fold(block):
    half = block.shape[0] // 2
    return jnp.concatenate([block[:half], block[half:]], axis=1)


def unfold(block):
    half = block.shape[1] // 2
    return jnp.concatenate([block[:, :half], block[:, half:]], axis=0)


def body(
    tokens, segment_ids, route_one, route_two, route_three, attn_gain, router,
    w_query, w_key, w_value, w_out, ffn_gain, w_gate, w_up, w_down, cotangent,
):
    nr, nc = lax.axis_size("row"), lax.axis_size("col")
    dr = w_query.shape[0]
    width = nr * dr
    qc, kc = w_query.shape[1], w_key.shape[1]
    fc = w_gate.shape[1]
    pairs = [(i, i ^ 1) for i in range(nc)]
    core = lax.axis_index("col") % 2

    att = fold(jnp.concatenate([w_query, w_key, w_value, w_out], axis=1))
    att_rows = att.shape[0]
    att = jnp.concatenate([att, pack_small(attn_gain, router, ffn_gain, att.shape[1])], axis=0)
    swapped = lax.ppermute(jnp.where(core == 0, w_up, w_gate), "col", pairs)
    gu = jnp.where(
        core == 0,
        jnp.concatenate([w_gate, swapped], axis=1),
        jnp.concatenate([swapped, w_up], axis=1),
    )
    dn = w_down.T
    att_all = lax.all_gather(att, ("col", "row"), axis=0)
    gu_all = lax.all_gather(gu, ("col", "row"), axis=0)
    dn_all = lax.all_gather(dn, ("row", "col"), axis=0)
    fw = 2 * fc
    gu_all = gu_all.reshape(nc // 2, 2, width, fw)
    dn_all = dn_all.reshape(nr, width, w_down.shape[0])
    att_all = att_all.reshape(nc, nr, *att.shape)
    small = att_all[0, :, att_rows:].reshape(nr, -1)[:, : 5 * dr].reshape(width, 5)
    small = small.astype(F32)
    gain_one, router_cols, gain_two = small[:, 0], small[:, 1:4], small[:, 4]
    aw = att_all[:, :, :att_rows].reshape(nc, nr, att_rows, 2, qc * 2 + kc * 2)
    aw = aw.transpose(1, 3, 2, 0, 4).reshape(width, nc, qc * 2 + kc * 2)
    full_query = aw[:, :, :qc].reshape(width, -1)
    full_key = aw[:, :, qc : qc + kc].reshape(width, -1)
    full_value = aw[:, :, qc + kc : qc + 2 * kc].reshape(width, -1)
    full_out = aw[:, :, qc + 2 * kc :].reshape(width, -1)

    routes = (route_one[0], route_two[0], route_three[0])
    counts = tuple(route.shape[0] for route in routes)
    chosen, where_at, segment, place = token_order(segment_ids[0], routes)
    stream = dot(chosen, tokens[0])
    grad_stream = dot(chosen, cotangent[0])
    half = HEAD_DIM // 2
    inverse = ROPE_BASE ** (-(jnp.arange(half, dtype=F32) * 2.0 / HEAD_DIM))
    angles = place[: counts[0]].astype(F32)[:, None] * inverse[None, :]
    cosine, sine = jnp.cos(angles), jnp.sin(angles)
    top = counts[0]
    allowed = (segment[None, :top] == segment[:top, None]) & (
        where_at[None, :top] <= where_at[:top, None]
    )

    kept = []
    for step in range(STEPS):
        rows = counts[step]
        picked = stream[:rows]
        gate_value = jax.nn.sigmoid(jnp.dot(picked, router_cols[:, step], precision=highest))
        inv_one = rms(picked)
        normed = (picked * inv_one * gain_one).astype(BF16)
        co, si = cosine[:rows], sine[:rows]
        query = dot(normed, full_query).reshape(rows, KV_HEADS, GROUPS, HEAD_DIM)
        key = dot(normed, full_key).reshape(rows, KV_HEADS, HEAD_DIM)
        value = dot(normed, full_value).astype(BF16).reshape(rows, KV_HEADS, HEAD_DIM)
        query = rotate(query, co[:, None, None, :], si[:, None, None, :]).astype(BF16)
        key = rotate(key, co[:, None, :], si[:, None, :]).astype(BF16)
        scores = jnp.einsum("qkgd,skd->kgqs", query, key, preferred_element_type=F32) * SCALE
        masked = jnp.where(allowed[:rows, :rows], scores, -1e30)
        row_max = jnp.max(masked, axis=-1, keepdims=True)
        expo = jnp.exp(masked - row_max)
        prob = expo / jnp.sum(expo, axis=-1, keepdims=True)
        prob_low = prob.astype(BF16)
        mixed = jnp.einsum("kgqs,skd->qkgd", prob_low, value, preferred_element_type=F32)
        mixed = mixed.reshape(rows, HEADS * HEAD_DIM).astype(BF16)
        attn_out = dot(mixed, full_out)
        middle = picked + attn_out
        inv_two = rms(middle)
        normed_two = (middle * inv_two * gain_two).astype(BF16)
        gates, ups, hiddens = [], [], []
        ffn_out = None
        for block in range(nc // 2):
            gate_raw = dot(normed_two, gu_all[block, 0])
            up_raw = dot(normed_two, gu_all[block, 1])
            gates.append(gate_raw)
            ups.append(up_raw)
            hidden = (jax.nn.silu(gate_raw) * up_raw).astype(BF16)
            hiddens.append(hidden)
            part = dot_nt(hidden, dn_all[block])
            ffn_out = part if ffn_out is None else ffn_out + part
        both = attn_out + ffn_out
        updated = picked + gate_value[:, None] * both
        stream = jnp.concatenate([updated, stream[rows:]], axis=0)
        kept.append(
            (picked, gate_value, inv_one, normed, query, key, value, prob, prob_low, mixed,
             middle, inv_two, normed_two, gates, ups, hiddens, both)
        )

    output = dot_tn(chosen, stream.astype(BF16)).astype(BF16)

    router_grads, gain_one_grad, gain_two_grad = [None] * STEPS, 0.0, 0.0
    stacks = [[] for _ in range(8)]
    per_block = [[[] for _ in range(nc // 2)] for _ in range(3)]
    for step in reversed(range(STEPS)):
        rows = counts[step]
        (picked, gate_value, inv_one, normed, query, key, value, prob, prob_low, mixed,
         middle, inv_two, normed_two, gates, ups, hiddens, both) = kept[step]
        co, si = cosine[:rows], sine[:rows]
        grad_new = grad_stream[:rows]
        grad_logit = jnp.sum(grad_new * both, axis=1) * gate_value * (1.0 - gate_value)
        grad_branch = gate_value[:, None] * grad_new
        grad_ffn = grad_branch.astype(BF16)
        grad_n2 = None
        for block in range(nc // 2):
            grad_hidden = dot(grad_ffn, dn_all[block])
            gate_raw, up_raw = gates[block], ups[block]
            sig = jax.nn.sigmoid(gate_raw)
            act = gate_raw * sig
            grad_up = (grad_hidden * act).astype(BF16)
            grad_gate = (grad_hidden * up_raw * (sig + act * (1.0 - sig))).astype(BF16)
            part = dot_nt(grad_gate, gu_all[block, 0]) + dot_nt(grad_up, gu_all[block, 1])
            grad_n2 = part if grad_n2 is None else grad_n2 + part
            per_block[0][block].append(grad_gate)
            per_block[1][block].append(grad_up)
            per_block[2][block].append(hiddens[block])
        gain_two_grad = gain_two_grad + jnp.sum(grad_n2 * middle * inv_two, axis=0)
        grad_middle = rms_back(middle, inv_two, gain_two, grad_n2)
        grad_attn = (grad_branch + grad_middle).astype(BF16)
        grad_mixed = dot_nt(grad_attn, full_out).astype(BF16)
        grad_mixed = grad_mixed.reshape(rows, KV_HEADS, GROUPS, HEAD_DIM)
        grad_prob = jnp.einsum("qkgd,skd->kgqs", grad_mixed, value, preferred_element_type=F32)
        grad_value = jnp.einsum("kgqs,qkgd->skd", prob_low, grad_mixed, preferred_element_type=F32)
        grad_value = grad_value.reshape(rows, -1).astype(BF16)
        row_dot = jnp.sum(prob * grad_prob, axis=-1, keepdims=True)
        grad_scores = (prob * (grad_prob - row_dot)).astype(BF16)
        grad_query = jnp.einsum("kgqs,skd->qkgd", grad_scores, key, preferred_element_type=F32)
        grad_key = jnp.einsum("kgqs,qkgd->skd", grad_scores, query, preferred_element_type=F32)
        grad_query = rotate(grad_query * SCALE, co[:, None, None, :], -si[:, None, None, :])
        grad_key = rotate(grad_key * SCALE, co[:, None, :], -si[:, None, :])
        grad_query = grad_query.reshape(rows, -1).astype(BF16)
        grad_key = grad_key.reshape(rows, -1).astype(BF16)
        grad_n1 = dot_nt(grad_query, full_query) + dot_nt(grad_key, full_key)
        grad_n1 = grad_n1 + dot_nt(grad_value, full_value)
        gain_one_grad = gain_one_grad + jnp.sum(grad_n1 * picked * inv_one, axis=0)
        grad_norm = rms_back(picked, inv_one, gain_one, grad_n1)
        router_grads[step] = jnp.dot(grad_logit, picked, precision=highest)
        grad_picked = (
            grad_new + grad_middle + grad_norm + grad_logit[:, None] * router_cols[:, step][None, :]
        )
        grad_stream = jnp.concatenate([grad_picked, grad_stream[rows:]], axis=0)
        for where, item in zip(
            stacks,
            (normed, grad_query, grad_key, grad_value, mixed, grad_attn, normed_two, grad_ffn),
        ):
            where.append(item)
    token_grad = dot_tn(chosen, grad_stream.astype(BF16)).astype(BF16)

    normed, grad_query, grad_key, grad_value, mixed, grad_attn, normed_two, grad_ffn = [
        jnp.concatenate(items, axis=0) for items in stacks
    ]
    gu_grads, dn_grads = [], []
    for block in range(nc // 2):
        grad_gate, grad_up, hidden = [
            jnp.concatenate(per_block[i][block], axis=0) for i in range(3)
        ]
        gu_grads.append(dot_tn(normed_two, grad_gate).astype(BF16))
        gu_grads.append(dot_tn(normed_two, grad_up).astype(BF16))
        dn_grads.append(dot_tn(grad_ffn, hidden).astype(BF16))
    gu_grads = jnp.concatenate(gu_grads, axis=0)
    dn_grads = jnp.concatenate(dn_grads, axis=0)
    gu_part = lax.psum_scatter(gu_grads, ("col", "row"), scatter_dimension=0, tiled=True)
    dn_part = lax.psum_scatter(dn_grads, ("row", "col"), scatter_dimension=0, tiled=True)

    grads = [
        dot_tn(normed, grad_query), dot_tn(normed, grad_key), dot_tn(normed, grad_value),
        dot_tn(mixed, grad_attn),
    ]
    grads = [g.astype(BF16).reshape(width, nc, -1) for g in grads]
    grads = jnp.concatenate(grads, axis=2).reshape(nr, 2, att_rows, nc, -1)
    grads = grads.transpose(3, 0, 2, 1, 4).reshape(nc, nr, att_rows, -1)
    small = jnp.stack([gain_one_grad, *router_grads, gain_two_grad], axis=1).astype(BF16)
    small = small.reshape(nr, 5 * dr)
    extra = (att.shape[0] - att_rows) * att.shape[1]
    small = jnp.pad(small, ((0, 0), (0, extra - 5 * dr))).reshape(nr, -1, att.shape[1])
    small = jnp.broadcast_to(small[None], (nc, *small.shape))
    grads = jnp.concatenate([grads, small], axis=2).reshape(-1, att.shape[1])
    att_part = lax.psum_scatter(grads, ("col", "row"), scatter_dimension=0, tiled=True)

    mine = att_part[:att_rows]
    mine = unfold(mine).astype(F32)
    small = att_part[att_rows:].reshape(-1)[: 5 * dr].reshape(dr, 5).astype(F32)
    first, second = gu_part[:, :fc], gu_part[:, fc:]
    got = lax.ppermute(jnp.where(core == 0, second, first), "col", pairs)
    gate_block = jnp.where(core == 0, first, got).astype(F32)
    up_block = jnp.where(core == 0, got, second).astype(F32)
    down_block = dn_part.T.astype(F32)
    return (
        output[None],
        token_grad[None],
        small[:, 0],
        small[:, 1:4],
        mine[:, :qc],
        mine[:, qc : qc + kc],
        mine[:, qc + kc : qc + 2 * kc],
        mine[:, qc + 2 * kc :],
        small[:, 4],
        gate_block,
        up_block,
        down_block,
    )


def solution(mesh):
    seq = P(("row", "col"), None, None)
    ids = P(("row", "col"), None)
    mat = P("row", "col")
    return jax.shard_map(
        body,
        mesh=mesh,
        in_specs=(
            seq, ids, ids, ids, ids, P("row"), P("row", None), mat, mat, mat, mat, P("row"),
            mat, mat, mat, seq,
        ),
        out_specs=(
            seq, seq, P("row"), P("row", None), mat, mat, mat, mat, P("row"), mat, mat, mat,
        ),
        check_vma=False,
    )
```

```python
import jax
import jax.numpy as jnp
from jax import lax
from jax.experimental import pallas as pl
from jax.experimental.pallas import tpu as pltpu
from jax.sharding import PartitionSpec as P


HEADS = 15
KV_HEADS = 5
GROUPS = 3
HEAD_DIM = 64
STEPS = 3
EPS = 1e-05
ROPE_BASE = 10000.0
SCALE = HEAD_DIM ** (-0.5)
F32 = jnp.float32
BF16 = jnp.bfloat16
highest = lax.Precision.HIGHEST


def dot(a, b):
    return jnp.dot(a, b, preferred_element_type=F32)


def dot_nt(a, b):
    return lax.dot_general(a, b, (((1,), (1,)), ((), ())), preferred_element_type=F32)


def dot_tn(a, b):
    return lax.dot_general(a, b, (((0,), (0,)), ((), ())), preferred_element_type=F32)


def rms(values):
    return lax.rsqrt(jnp.mean(values * values, axis=-1, keepdims=True) + EPS)


def rms_back(values, inverse, gain, grad):
    scaled = grad * gain
    inner = jnp.mean(scaled * values, axis=-1, keepdims=True)
    return inverse * scaled - values * (inverse * inverse * inverse * inner)


def rotate(values, cosine, sine):
    half = HEAD_DIM // 2
    a, b = values[..., :half], values[..., half:]
    return jnp.concatenate([a * cosine - b * sine, b * cosine + a * sine], axis=-1)


def token_order(segment_row, routes):
    length = segment_row.shape[0]
    places = jnp.arange(length, dtype=jnp.int32)
    level = jnp.zeros((length,), jnp.int32)
    for route in routes:
        level = level + jnp.sum((route[:, None] == places[None, :]).astype(jnp.int32), axis=0)
    before = (level[:, None] > level[None, :]) | (
        (level[:, None] == level[None, :]) & (places[:, None] < places[None, :])
    )
    spot = jnp.sum(before.astype(jnp.int32), axis=0)
    earlier = (segment_row[:, None] == segment_row[None, :]) & (places[:, None] < places[None, :])
    place = jnp.sum(earlier.astype(jnp.int32), axis=0)
    chosen = spot[None, :] == places[:, None]
    zero = jnp.int32(0)
    pick = lambda v: jnp.sum(jnp.where(chosen, v[None, :], zero), axis=1)
    return chosen.astype(BF16), pick(places), pick(segment_row), pick(place)


def pack_small(attn_gain, router, ffn_gain, width):
    flat = jnp.concatenate([attn_gain[:, None], router, ffn_gain[:, None]], axis=1).reshape(-1)
    rows = -(-flat.shape[0] // width)
    rows = -(-rows // 8) * 8
    return jnp.pad(flat, (0, rows * width - flat.shape[0])).reshape(rows, width)


def fold(block):
    half = block.shape[0] // 2
    return jnp.concatenate([block[:half], block[half:]], axis=1)


def unfold(block):
    half = block.shape[1] // 2
    return jnp.concatenate([block[:, :half], block[:, half:]], axis=0)


def to_x(value):
    return lax.ppermute(value, "row", [(i, i ^ 1) for i in range(4)])


def to_y(value):
    return lax.ppermute(value, "row", [(i, i ^ 2) for i in range(4)])


def to_core(value):
    return lax.ppermute(value, "col", [(i, i ^ 1) for i in range(8)])


def to_up(value, low, high):
    return lax.ppermute(value, "col", [(i, i + 2) for i in range(2 * low, 2 * high + 2)])


def to_down(value, low, high):
    return lax.ppermute(value, "col", [(i, i - 2) for i in range(2 * low, 2 * high + 2)])


def add_low(*values):
    total = values[0].astype(F32)
    for value in values[1:]:
        total = total + value.astype(F32)
    return total.astype(BF16)


def place_kernel(cuts, first, where, *refs):
    sources = refs[:10]
    outs = refs[10 if first else 13 :][:3]
    bufs, sem_in, sem_out = refs[-5:-2], refs[-2], refs[-1]
    plane, row, core = where[0], where[1], where[2]
    arrivals, leaves = [], []
    for side in range(2):
        p, a, b, dx, dy = sources[side * 5 : side * 5 + 5]
        for rel in range(4):
            slot = side * 4 + rel
            for part in range(3):
                low, high = cuts[part], cuts[part + 1]
                if rel < 3:
                    src = (p, a, b)[rel].at[pl.ds(low, high - low)]
                elif part < 2:
                    src = dx.at[pl.ds(low, high - low)]
                else:
                    src = dy
                k = slot * 3 + part
                arrivals.append(pltpu.make_async_copy(src, bufs[part].at[slot], sem_in.at[k]))
                r = jnp.bitwise_xor(row, rel)
                c = jnp.bitwise_xor(core, side)
                dst = outs[part].at[r, plane, c] if part == 1 else outs[part].at[plane, c, r]
                leaves.append(pltpu.make_async_copy(bufs[part].at[slot], dst, sem_out.at[k]))
    for copy in arrivals:
        copy.start()
    for arrive, leave in zip(arrivals, leaves):
        arrive.wait()
        leave.start()
    for copy in leaves:
        copy.wait()


def place(cuts, where, sources, held):
    width = sources[0].shape[1]
    sizes = [high - low for low, high in zip(cuts, cuts[1:])]
    shapes = [(4, 2, 4, sizes[0], width), (4, 4, 2, sizes[1], width), (4, 2, 4, sizes[2], width)]
    first = held is None
    anywhere = pl.BlockSpec(memory_space=pl.ANY)
    inputs = list(sources) + ([] if first else list(held))
    return pl.pallas_call(
        lambda *refs: place_kernel(cuts, first, *refs),
        grid_spec=pltpu.PrefetchScalarGridSpec(
            num_scalar_prefetch=1,
            grid=(1,),
            in_specs=[anywhere] * len(inputs),
            out_specs=[anywhere] * 3,
            scratch_shapes=[pltpu.VMEM((8, n, width), BF16) for n in sizes]
            + [pltpu.SemaphoreType.DMA((24,)), pltpu.SemaphoreType.DMA((24,))],
        ),
        out_shape=[jax.ShapeDtypeStruct(shape, BF16) for shape in shapes],
        input_output_aliases={} if first else {11: 0, 12: 1, 13: 2},
        compiler_params=pltpu.CompilerParams(vmem_limit_bytes=24 << 20),
        cost_estimate=pl.CostEstimate(flops=0, bytes_accessed=10 << 20, transcendentals=0),
        name="place",
    )(where, *inputs)


def gather_units(unit, cuts):
    half = cuts[2]
    z, core = lax.axis_index("col") // 2, lax.axis_index("col") % 2
    row = lax.axis_index("row")
    u, d = [unit], [unit]
    for hop in range(3):
        u.append(to_up(u[-1], hop, 2))
        d.append(to_down(d[-1], 1, 3 - hop))
    p1 = jnp.where((z == 3) | (z == 1), u[1], d[1])
    u1, d1, _ = lax.optimization_barrier((u[1], d[1], p1))
    p2 = jnp.where(z == 0, d[2], jnp.where(z == 1, d1, jnp.where(z == 2, u1, u[2])))
    u2, d2, _ = lax.optimization_barrier((u[2], d[2], p2))
    p3 = jnp.where(z == 0, d[3], jnp.where(z == 1, d2, jnp.where(z == 2, u2, u[3])))
    order = jnp.array([[0, 1, 2, 3], [1, 0, 2, 3], [2, 3, 1, 0], [3, 2, 1, 0]], jnp.int32)[z]
    held = None
    for i, p in enumerate((unit, p1, p2, p3)):
        a, b = to_x(p), to_y(p)
        dx, dy = to_x(b[:half]), to_y(a[half:])
        if i == 0:
            dx, dy, _, _ = lax.optimization_barrier((dx, dy, u[3], d[3]))
        if i == 1:
            dx, dy, _ = lax.optimization_barrier((dx, dy, p3))
        mine = (p, a, b, dx, dy)
        other = [to_core(v) for v in mine]
        where = jnp.stack([order[i], row, core]).astype(jnp.int32)
        held = place(cuts, where, [*mine, *other], held)
    return held


def pick_kernel(cuts, where, *refs):
    sources, outs = refs[:3], refs[3:5]
    bufs, sem_in, sem_out = refs[-5:-2], refs[-2], refs[-1]
    plane, row, core = where[0], where[1], where[2]
    arrivals, leaves = [], []
    for side in (1, 0):
        for rel in range(4):
            slot = side * 4 + rel
            r = jnp.bitwise_xor(row, rel)
            c = jnp.bitwise_xor(core, side)
            for part in range(3):
                low, high = cuts[part], cuts[part + 1]
                k = slot * 3 + part
                src = sources[part]
                src = src.at[r, plane, c] if part == 1 else src.at[plane, c, r]
                arrivals.append(pltpu.make_async_copy(src, bufs[part].at[slot], sem_in.at[k]))
                dst = outs[side].at[rel, pl.ds(low, high - low)]
                leaves.append(pltpu.make_async_copy(bufs[part].at[slot], dst, sem_out.at[k]))
    for copy in arrivals:
        copy.start()
    for arrive, leave in zip(arrivals, leaves):
        arrive.wait()
        leave.start()
    for copy in leaves:
        copy.wait()


def pick(cuts, where, sources):
    width = sources[0].shape[-1]
    sizes = [high - low for low, high in zip(cuts, cuts[1:])]
    anywhere = pl.BlockSpec(memory_space=pl.ANY)
    return pl.pallas_call(
        lambda *refs: pick_kernel(cuts, *refs),
        grid_spec=pltpu.PrefetchScalarGridSpec(
            num_scalar_prefetch=1,
            grid=(1,),
            in_specs=[anywhere] * 3,
            out_specs=[anywhere] * 2,
            scratch_shapes=[pltpu.VMEM((8, n, width), BF16) for n in sizes]
            + [pltpu.SemaphoreType.DMA((24,)), pltpu.SemaphoreType.DMA((24,))],
        ),
        out_shape=[jax.ShapeDtypeStruct((4, cuts[3], width), BF16)] * 2,
        compiler_params=pltpu.CompilerParams(vmem_limit_bytes=24 << 20),
        cost_estimate=pl.CostEstimate(flops=0, bytes_accessed=10 << 20, transcendentals=0),
        name="pick",
    )(where, *sources)


def reduce_units(parts, cuts):
    half = cuts[2]
    z, core = lax.axis_index("col") // 2, lax.axis_index("col") % 2
    row = lax.axis_index("row")
    order = jnp.array([[3, 2, 1, 0], [3, 2, 0, 1], [0, 1, 3, 2], [0, 1, 2, 3]], jnp.int32)[z]
    sums = []
    for i in range(4):
        where = jnp.stack([order[i], row, core]).astype(jnp.int32)
        mine, other = pick(cuts, where, parts)
        g = add_low(mine, to_core(other))
        dx, dy = to_x(g[3][:half]), to_y(g[3][half:])
        for_x = jnp.concatenate([g[1][:half], add_low(g[1][half:], dy)], axis=0)
        for_y = jnp.concatenate([add_low(g[2][:half], dx), g[2][half:]], axis=0)
        ax, ay = to_x(for_x), to_y(for_y)
        sums.append(add_low(g[0], ax, ay))
    one, two, three, own = sums
    u, d = to_up(one, 0, 0), to_down(one, 3, 3)
    u = to_up(add_low(jnp.where(z == 0, two, one), u), 0, 1)
    d = to_down(add_low(jnp.where(z == 3, two, one), d), 2, 3)
    u = to_up(add_low(jnp.where(z == 1, two, three), u), 0, 2)
    d = to_down(add_low(jnp.where(z == 2, two, three), d), 1, 3)
    return own.astype(F32) + u.astype(F32) + d.astype(F32)


def body(
    tokens, segment_ids, route_one, route_two, route_three, attn_gain, router,
    w_query, w_key, w_value, w_out, ffn_gain, w_gate, w_up, w_down, cotangent,
):
    nr, nc = lax.axis_size("row"), lax.axis_size("col")
    dr = w_query.shape[0]
    width = nr * dr
    qc, kc = w_query.shape[1], w_key.shape[1]
    fc = w_gate.shape[1]
    pairs = [(i, i ^ 1) for i in range(nc)]
    core = lax.axis_index("col") % 2

    att = fold(jnp.concatenate([w_query, w_key, w_value, w_out], axis=1))
    att_rows = att.shape[0]
    att = jnp.concatenate([att, pack_small(attn_gain, router, ffn_gain, att.shape[1])], axis=0)
    swapped = lax.ppermute(jnp.where(core == 0, w_up, w_gate), "col", pairs)
    gu = jnp.where(
        core == 0,
        jnp.concatenate([w_gate, swapped], axis=1),
        jnp.concatenate([swapped, w_up], axis=1),
    )
    dn = w_down.T
    cuts = (0, att.shape[0], att.shape[0] + dn.shape[0], att.shape[0] + dn.shape[0] + gu.shape[0])
    direct = (nr, nc) == (4, 8)
    if direct:
        att_all, dn_all, gu_all = gather_units(jnp.concatenate([att, dn, gu], axis=0), cuts)
    else:
        att_all = lax.all_gather(att, ("col", "row"), axis=0)
        gu_all = lax.all_gather(gu, ("col", "row"), axis=0)
        dn_all = lax.all_gather(dn, ("row", "col"), axis=0)
    fw = 2 * fc
    gu_all = gu_all.reshape(nc // 2, 2, width, fw)
    dn_all = dn_all.reshape(nr, width, w_down.shape[0])
    att_all = att_all.reshape(nc, nr, *att.shape)
    small = att_all[0, :, att_rows:].reshape(nr, -1)[:, : 5 * dr].reshape(width, 5)
    small = small.astype(F32)
    gain_one, router_cols, gain_two = small[:, 0], small[:, 1:4], small[:, 4]
    aw = att_all[:, :, :att_rows].reshape(nc, nr, att_rows, 2, qc * 2 + kc * 2)
    aw = aw.transpose(1, 3, 2, 0, 4).reshape(width, nc, qc * 2 + kc * 2)
    full_query = aw[:, :, :qc].reshape(width, -1)
    full_key = aw[:, :, qc : qc + kc].reshape(width, -1)
    full_value = aw[:, :, qc + kc : qc + 2 * kc].reshape(width, -1)
    full_out = aw[:, :, qc + 2 * kc :].reshape(width, -1)

    routes = (route_one[0], route_two[0], route_three[0])
    counts = tuple(route.shape[0] for route in routes)
    chosen, where_at, segment, place = token_order(segment_ids[0], routes)
    stream = dot(chosen, tokens[0])
    grad_stream = dot(chosen, cotangent[0])
    half = HEAD_DIM // 2
    inverse = ROPE_BASE ** (-(jnp.arange(half, dtype=F32) * 2.0 / HEAD_DIM))
    angles = place[: counts[0]].astype(F32)[:, None] * inverse[None, :]
    cosine, sine = jnp.cos(angles), jnp.sin(angles)
    top = counts[0]
    allowed = (segment[None, :top] == segment[:top, None]) & (
        where_at[None, :top] <= where_at[:top, None]
    )

    kept = []
    for step in range(STEPS):
        rows = counts[step]
        picked = stream[:rows]
        gate_value = jax.nn.sigmoid(jnp.dot(picked, router_cols[:, step], precision=highest))
        inv_one = rms(picked)
        normed = (picked * inv_one * gain_one).astype(BF16)
        co, si = cosine[:rows], sine[:rows]
        query = dot(normed, full_query).reshape(rows, KV_HEADS, GROUPS, HEAD_DIM)
        key = dot(normed, full_key).reshape(rows, KV_HEADS, HEAD_DIM)
        value = dot(normed, full_value).astype(BF16).reshape(rows, KV_HEADS, HEAD_DIM)
        query = rotate(query, co[:, None, None, :], si[:, None, None, :]).astype(BF16)
        key = rotate(key, co[:, None, :], si[:, None, :]).astype(BF16)
        scores = jnp.einsum("qkgd,skd->kgqs", query, key, preferred_element_type=F32) * SCALE
        masked = jnp.where(allowed[:rows, :rows], scores, -1e30)
        row_max = jnp.max(masked, axis=-1, keepdims=True)
        expo = jnp.exp(masked - row_max)
        prob = expo / jnp.sum(expo, axis=-1, keepdims=True)
        prob_low = prob.astype(BF16)
        mixed = jnp.einsum("kgqs,skd->qkgd", prob_low, value, preferred_element_type=F32)
        mixed = mixed.reshape(rows, HEADS * HEAD_DIM).astype(BF16)
        attn_out = dot(mixed, full_out)
        middle = picked + attn_out
        inv_two = rms(middle)
        normed_two = (middle * inv_two * gain_two).astype(BF16)
        gates, ups, hiddens = [], [], []
        ffn_out = None
        for block in range(nc // 2):
            gate_raw = dot(normed_two, gu_all[block, 0])
            up_raw = dot(normed_two, gu_all[block, 1])
            gates.append(gate_raw)
            ups.append(up_raw)
            hidden = (jax.nn.silu(gate_raw) * up_raw).astype(BF16)
            hiddens.append(hidden)
            part = dot_nt(hidden, dn_all[block])
            ffn_out = part if ffn_out is None else ffn_out + part
        both = attn_out + ffn_out
        updated = picked + gate_value[:, None] * both
        stream = jnp.concatenate([updated, stream[rows:]], axis=0)
        kept.append(
            (picked, gate_value, inv_one, normed, query, key, value, prob, prob_low, mixed,
             middle, inv_two, normed_two, gates, ups, hiddens, both)
        )

    output = dot_tn(chosen, stream.astype(BF16)).astype(BF16)

    router_grads, gain_one_grad, gain_two_grad = [None] * STEPS, 0.0, 0.0
    stacks = [[] for _ in range(8)]
    per_block = [[[] for _ in range(nc // 2)] for _ in range(3)]
    for step in reversed(range(STEPS)):
        rows = counts[step]
        (picked, gate_value, inv_one, normed, query, key, value, prob, prob_low, mixed,
         middle, inv_two, normed_two, gates, ups, hiddens, both) = kept[step]
        co, si = cosine[:rows], sine[:rows]
        grad_new = grad_stream[:rows]
        grad_logit = jnp.sum(grad_new * both, axis=1) * gate_value * (1.0 - gate_value)
        grad_branch = gate_value[:, None] * grad_new
        grad_ffn = grad_branch.astype(BF16)
        grad_n2 = None
        for block in range(nc // 2):
            grad_hidden = dot(grad_ffn, dn_all[block])
            gate_raw, up_raw = gates[block], ups[block]
            sig = jax.nn.sigmoid(gate_raw)
            act = gate_raw * sig
            grad_up = (grad_hidden * act).astype(BF16)
            grad_gate = (grad_hidden * up_raw * (sig + act * (1.0 - sig))).astype(BF16)
            part = dot_nt(grad_gate, gu_all[block, 0]) + dot_nt(grad_up, gu_all[block, 1])
            grad_n2 = part if grad_n2 is None else grad_n2 + part
            per_block[0][block].append(grad_gate)
            per_block[1][block].append(grad_up)
            per_block[2][block].append(hiddens[block])
        gain_two_grad = gain_two_grad + jnp.sum(grad_n2 * middle * inv_two, axis=0)
        grad_middle = rms_back(middle, inv_two, gain_two, grad_n2)
        grad_attn = (grad_branch + grad_middle).astype(BF16)
        grad_mixed = dot_nt(grad_attn, full_out).astype(BF16)
        grad_mixed = grad_mixed.reshape(rows, KV_HEADS, GROUPS, HEAD_DIM)
        grad_prob = jnp.einsum("qkgd,skd->kgqs", grad_mixed, value, preferred_element_type=F32)
        grad_value = jnp.einsum("kgqs,qkgd->skd", prob_low, grad_mixed, preferred_element_type=F32)
        grad_value = grad_value.reshape(rows, -1).astype(BF16)
        row_dot = jnp.sum(prob * grad_prob, axis=-1, keepdims=True)
        grad_scores = (prob * (grad_prob - row_dot)).astype(BF16)
        grad_query = jnp.einsum("kgqs,skd->qkgd", grad_scores, key, preferred_element_type=F32)
        grad_key = jnp.einsum("kgqs,qkgd->skd", grad_scores, query, preferred_element_type=F32)
        grad_query = rotate(grad_query * SCALE, co[:, None, None, :], -si[:, None, None, :])
        grad_key = rotate(grad_key * SCALE, co[:, None, :], -si[:, None, :])
        grad_query = grad_query.reshape(rows, -1).astype(BF16)
        grad_key = grad_key.reshape(rows, -1).astype(BF16)
        grad_n1 = dot_nt(grad_query, full_query) + dot_nt(grad_key, full_key)
        grad_n1 = grad_n1 + dot_nt(grad_value, full_value)
        gain_one_grad = gain_one_grad + jnp.sum(grad_n1 * picked * inv_one, axis=0)
        grad_norm = rms_back(picked, inv_one, gain_one, grad_n1)
        router_grads[step] = jnp.dot(grad_logit, picked, precision=highest)
        grad_picked = (
            grad_new + grad_middle + grad_norm + grad_logit[:, None] * router_cols[:, step][None, :]
        )
        grad_stream = jnp.concatenate([grad_picked, grad_stream[rows:]], axis=0)
        for where, item in zip(
            stacks,
            (normed, grad_query, grad_key, grad_value, mixed, grad_attn, normed_two, grad_ffn),
        ):
            where.append(item)
    token_grad = dot_tn(chosen, grad_stream.astype(BF16)).astype(BF16)

    normed, grad_query, grad_key, grad_value, mixed, grad_attn, normed_two, grad_ffn = [
        jnp.concatenate(items, axis=0) for items in stacks
    ]
    gu_grads, dn_grads = [], []
    for block in range(nc // 2):
        grad_gate, grad_up, hidden = [
            jnp.concatenate(per_block[i][block], axis=0) for i in range(3)
        ]
        gu_grads.append(dot_tn(normed_two, grad_gate).astype(BF16))
        gu_grads.append(dot_tn(normed_two, grad_up).astype(BF16))
        dn_grads.append(dot_tn(grad_ffn, hidden).astype(BF16))
    gu_grads = jnp.concatenate(gu_grads, axis=0)
    dn_grads = jnp.concatenate(dn_grads, axis=0)
    grads = [
        dot_tn(normed, grad_query), dot_tn(normed, grad_key), dot_tn(normed, grad_value),
        dot_tn(mixed, grad_attn),
    ]
    grads = [g.astype(BF16).reshape(width, nc, -1) for g in grads]
    grads = jnp.concatenate(grads, axis=2).reshape(nr, 2, att_rows, nc, -1)
    grads = grads.transpose(3, 0, 2, 1, 4).reshape(nc, nr, att_rows, -1)
    small = jnp.stack([gain_one_grad, *router_grads, gain_two_grad], axis=1).astype(BF16)
    small = small.reshape(nr, 5 * dr)
    extra = (att.shape[0] - att_rows) * att.shape[1]
    small = jnp.pad(small, ((0, 0), (0, extra - 5 * dr))).reshape(nr, -1, att.shape[1])
    small = jnp.broadcast_to(small[None], (nc, *small.shape))
    grads = jnp.concatenate([grads, small], axis=2).reshape(-1, att.shape[1])
    if direct:
        parts = (
            grads.reshape(4, 2, 4, -1, fw),
            dn_grads.reshape(4, 4, 2, -1, fw),
            gu_grads.reshape(4, 2, 4, -1, fw),
        )
        total = reduce_units(parts, cuts)
        att_part, dn_part, gu_part = [total[a:b] for a, b in zip(cuts, cuts[1:])]
    else:
        att_part = lax.psum_scatter(grads, ("col", "row"), scatter_dimension=0, tiled=True)
        gu_part = lax.psum_scatter(gu_grads, ("col", "row"), scatter_dimension=0, tiled=True)
        dn_part = lax.psum_scatter(dn_grads, ("row", "col"), scatter_dimension=0, tiled=True)

    mine = att_part[:att_rows]
    mine = unfold(mine).astype(F32)
    small = att_part[att_rows:].reshape(-1)[: 5 * dr].reshape(dr, 5).astype(F32)
    first, second = gu_part[:, :fc], gu_part[:, fc:]
    got = lax.ppermute(jnp.where(core == 0, second, first).astype(BF16), "col", pairs)
    first, second, got = first.astype(F32), second.astype(F32), got.astype(F32)
    gate_block = jnp.where(core == 0, first, got)
    up_block = jnp.where(core == 0, got, second)
    down_block = dn_part.T.astype(F32)
    return (
        output[None],
        token_grad[None],
        small[:, 0],
        small[:, 1:4],
        mine[:, :qc],
        mine[:, qc : qc + kc],
        mine[:, qc + kc : qc + 2 * kc],
        mine[:, qc + 2 * kc :],
        small[:, 4],
        gate_block,
        up_block,
        down_block,
    )


def solution(mesh):
    seq = P(("row", "col"), None, None)
    ids = P(("row", "col"), None)
    mat = P("row", "col")
    return jax.shard_map(
        body,
        mesh=mesh,
        in_specs=(
            seq, ids, ids, ids, ids, P("row"), P("row", None), mat, mat, mat, mat, P("row"),
            mat, mat, mat, seq,
        ),
        out_specs=(
            seq, seq, P("row"), P("row", None), mat, mat, mat, mat, P("row"), mat, mat, mat,
        ),
        check_vma=False,
    )
```
